128 devices in a mesh: band: 8 (over z, core), trial: 16 (over y, x).
Axes of the slice: x: 4, y: 4, z: 4, core: 2. Of those that a mesh axis runs over, the one named last changes fastest.
Arguments:
- intensity: bfloat16 [2, 16384, 4096], P(None, 'band', 'trial'), may hold values from -6 to 6
- fine_delay: int32 [32, 32, 512], P('band'), may hold values from 0 to 31
- span_start: int32 [16, 32], replicated, may hold values from 0 to 28
- sub_rel: int32 [1024, 32], P('trial'), may hold values from 0 to 3
- offset: int32 [1024, 32], P('trial'), may hold values from 0 to 2048
- widths: int32 [4], replicated, may hold values from 1 to 64
Outputs:
- series: bfloat16 [2, 1024, 4096], P(None, ('trial', 'band'))
- peaks: float32 [2, 1024, 4], P(None, ('trial', 'band'))
The draws below stay inside these ranges and needn't reach their ends.
All inputs are finite; a program needn't handle non-finite values.
Results may differ from the reference program's by a relative error of at most 0.014.
Values may be sent and summed in bfloat16 or wider, within the bound.
A program may use at most 64 MiB of HBM per device.

```python
import math
import jax
import jax.numpy as jnp
from jax import lax

BEAMS = 2
CH = 16384
SUBS = 32
CSUB = 512
Q = 32
QSPAN = 4
MAXD1 = 32
TIME = 4096
MAXD2 = 2048
TRIAL_DEV = 64
TRIALS = 1024
NW = 4
MAXW = 64
N_TRIAL = 16


def plant(values, own_key, smallest, largest):
    spot = [jax.random.randint(jax.random.fold_in(own_key, axis), (), 0, length) for axis, length in enumerate(values.shape)]
    widest = values.shape.index(max(values.shape))
    beside = spot[:widest] + [(spot[widest] + 1) % values.shape[widest]] + spot[widest + 1:]
    return values.at[tuple(spot)].set(smallest).at[tuple(beside)].set(largest)


def shard_levels(key, dims, cuts, smallest, top_value):
    factor_of = 1.0
    for axis_at, blocks in cuts:
        steps = jax.random.uniform(jax.random.fold_in(jax.random.fold_in(key, 6), axis_at), (blocks,), jnp.float32, smallest / len(cuts), top_value / len(cuts))
        factor_of = factor_of * jnp.repeat(jnp.exp(steps), dims[axis_at] // blocks).reshape((-1,) + (1,) * (len(dims) - 1 - axis_at))
    return factor_of


def gaussian(rng, dims, deviation, reach, pieces=(), kind=jnp.bfloat16):
    drawn = jax.random.normal(rng, dims, jnp.float32) * deviation
    if len(pieces) > 0:
        drawn = shard_levels(rng, dims, pieces, -0.22, 0.18) * drawn
    return jnp.clip(drawn, min=-reach, max=reach).astype(kind)


def setup_inputs(seed: int = 0) -> dict:
    key_of = jax.random.split(jax.random.key(seed), 7)
    intensity = gaussian(key_of[0], (BEAMS, CH, TIME), 1.0, 6.0, ((1, 8), (2, 16)))
    fine_delay = plant(jax.random.randint(key_of[1], (SUBS, Q, CSUB), 0, MAXD1), jax.random.fold_in(key_of[1], 1), 0, MAXD1 - 1).astype(jnp.int32)
    span_start = plant(jax.random.randint(key_of[2], (N_TRIAL, SUBS), 0, Q - QSPAN + 1), jax.random.fold_in(key_of[2], 1), 0, Q - QSPAN).astype(jnp.int32)
    sub_rel = plant(jax.random.randint(key_of[3], (TRIALS, SUBS), 0, QSPAN), jax.random.fold_in(key_of[3], 1), 0, QSPAN - 1).astype(jnp.int32)
    offset = plant(jax.random.randint(key_of[4], (TRIALS, SUBS), 0, MAXD2 + 1), jax.random.fold_in(key_of[4], 1), 0, MAXD2).astype(jnp.int32)
    widths = plant(jax.random.randint(key_of[5], (NW,), 1, MAXW + 1), jax.random.fold_in(key_of[5], 1), 1, MAXW).astype(jnp.int32)
    return {"intensity": intensity, "fine_delay": fine_delay, "span_start": span_start, "sub_rel": sub_rel, "offset": offset, "widths": widths}


def boxcar_peaks(series, widths):
    values = series.astype(jnp.float32)
    length = values.shape[2]
    running = jnp.cumsum(values, axis=2)
    start_zero = jnp.zeros(values.shape[:2] + (1,), jnp.float32)
    tail_sums = jnp.broadcast_to(running[:, :, -1:], values.shape[:2] + (MAXW,))
    prefix_sums = jnp.concatenate([start_zero, running, tail_sums], axis=2)
    peak_list = []
    for width_slot in range(widths.shape[0]):
        width_now = widths[width_slot]
        upper_sums = lax.dynamic_slice_in_dim(prefix_sums, width_now, length, 2)
        boxcar_sums = (upper_sums - prefix_sums[:, :, :length]) / jnp.sqrt(width_now.astype(jnp.float32))
        peak_list.append(lax.optimization_barrier(jnp.max(boxcar_sums, axis=2)))
    return jnp.stack(peak_list, axis=2)

def reference(intensity, fine_delay, span_start, sub_rel, offset, widths):
    blocks = intensity.reshape(BEAMS, SUBS, CSUB, TIME).transpose(1, 0, 2, 3)

    def sub_band(operands):
        block_data, delays = operands
        extended = jnp.pad(block_data.astype(jnp.float32), ((0, 0), (0, 0), (0, MAXD1)))
        summed_band = jnp.zeros((BEAMS, Q, TIME), jnp.float32)
        for delay_step in range(MAXD1):
            selector = (delays == delay_step).astype(jnp.float32)
            summed_band = summed_band + jnp.einsum('qc,bct->bqt', selector, extended[:, :, delay_step:delay_step + TIME], precision=lax.Precision.HIGHEST)
        return summed_band.astype(jnp.bfloat16)
    partial_rows = lax.map(sub_band, (blocks, fine_delay))
    padded = jnp.pad(partial_rows, ((0, 0), (0, 0), (0, 0), (0, MAXD2)))
    trial_range = jnp.arange(TRIALS, dtype=jnp.int32) // TRIAL_DEV
    sub_trial = (span_start[trial_range] + sub_rel).astype(jnp.int32)
    band_index = jnp.arange(SUBS, dtype=jnp.int32)

    def select(band_id, row_start, time_shift):
        zero_index = jnp.zeros((), jnp.int32)
        picked = lax.dynamic_slice(padded, (band_id, zero_index, row_start, time_shift), (1, BEAMS, 1, TIME))
        return picked[0, :, 0].astype(jnp.float32)

    def one_trial(rows_one, shifts_one):
        return lax.optimization_barrier(jnp.sum(jax.vmap(select)(band_index, rows_one, shifts_one), axis=0))
    groups = TRIALS // 8

    def trial_group(operands):
        return jax.vmap(one_trial)(operands[0], operands[1])
    summed = lax.map(trial_group, (sub_trial.reshape(groups, 8, SUBS), offset.reshape(groups, 8, SUBS)))
    summed = summed.reshape(TRIALS, BEAMS, TIME).transpose(1, 0, 2)
    series = (summed / math.sqrt(CH)).astype(jnp.bfloat16)
    return (series, boxcar_peaks(series, widths))
```

```python
import math

import jax
import jax.numpy as jnp
from jax import lax
from jax.experimental import pallas as pl
from jax.experimental.pallas import tpu as pltpu
from jax.sharding import PartitionSpec as P

CH = 16384
QSPAN = 4
MAXD1 = 32
MAXD2 = 2048
LANES = 128
NT = 16
SUBS = 4
CSUB = 512
Q = 32
BLOCK = 256
ROWS = 32
PITCH = ROWS + MAXD2 // LANES + 1
MSG = 80
MESH = pl.DeviceIdType.MESH


def shift_add(first, second, step, lane):
    keep = lane < LANES - step
    low = pltpu.roll(second[1], LANES - step, 1)
    high = pltpu.roll(second[2], LANES - step, 1)
    if second[0] is None:
        early = jnp.where(keep, 0.0, low)
    else:
        early = jnp.where(keep, pltpu.roll(second[0], LANES - step, 1), low)
    if first[0] is not None:
        early = early + first[0]
    return (
        early,
        first[1] + jnp.where(keep, low, high),
        first[2] + jnp.where(keep, high, 0.0),
    )


def kernel(
    x_hbm, delay_hbm, span_ref, rel_ref, off_ref, width_ref,
    series_ref, peaks_ref,
    xv, dv, sel, lag, part, send, recv, rows, relay, chunk, half, near, total, flat, window,
    in_sem, send_sem, recv_sem, fsend_sem, frecv_sem, zsend_sem, zrecv_sem,
):
    band = lax.axis_index("band")
    me = lax.axis_index("trial")
    z = lax.div(band, 2)
    core = lax.rem(band, 2)
    sibling = band + 1 - 2 * core
    up = lax.rem(band + 2, 8)
    down = lax.rem(band + 6, 8)

    barrier = pltpu.get_barrier_semaphore()

    def greet(i, carry):
        pl.semaphore_signal(barrier, inc=1, device_id={"trial": lax.rem(me + i, NT)}, device_id_type=MESH)
        return carry

    lax.fori_loop(1, NT, greet, 0)
    for other in (sibling, up, down):
        pl.semaphore_signal(barrier, inc=1, device_id={"band": other}, device_id_type=MESH)

    def load(s):
        cut = pl.ds(s * CSUB, CSUB)
        return (
            pltpu.make_async_copy(x_hbm.at[:, cut, :], xv.at[:, cut, :], in_sem.at[0, s]),
            pltpu.make_async_copy(delay_hbm.at[s], dv.at[s], in_sem.at[1, s]),
        )

    for s in range(SUBS):
        for copy in load(s):
            copy.start()

    lane = lax.broadcasted_iota(jnp.int32, (8, LANES), 1)
    rows[...] = jnp.zeros_like(rows)
    recv[0, NT] = jnp.zeros_like(recv[0, NT])
    recv[1, NT] = jnp.zeros_like(recv[1, NT])
    flat[...] = jnp.zeros_like(flat)

    ahead = lax.broadcasted_iota(jnp.int32, (2 * LANES, LANES), 0) - lax.broadcasted_iota(
        jnp.int32, (2 * LANES, LANES), 1
    )
    for w in range(4):
        inside = (ahead >= 0) & (ahead < width_ref[w])
        window[:, w * LANES : (w + 1) * LANES] = jnp.where(inside, 1.0, 0.0).astype(jnp.bfloat16)

    for s in range(SUBS):
        for copy in load(s):
            copy.wait()
        delays = dv[s].astype(jnp.float32).astype(jnp.bfloat16)
        one = jnp.ones((), jnp.bfloat16)
        zero = jnp.zeros((), jnp.bfloat16)
        for k in range(MAXD1):
            sel[k * Q : (k + 1) * Q, :] = jnp.where(delays == jnp.bfloat16(k), one, zero)
        for b in range(2):
            lag[b] = jnp.dot(
                sel[...], xv[b, s * CSUB : (s + 1) * CSUB, :], preferred_element_type=jnp.float32
            )

        def tree(step, carry):
            b = lax.div(step, 4)
            group = lax.rem(step, 4)

            def node(level, k):
                if level == 0:
                    at = pl.ds(pl.multiple_of(k * Q + group * 8, 8), 8)
                    return (None, lag[b, at, 0:LANES], lag[b, at, LANES : 2 * LANES])
                stride = MAXD1 >> level
                return shift_add(node(level - 1, k), node(level - 1, k + stride), stride, lane)

            early, low, high = node(5, 0)
            at = pl.ds(s * 64 + group * 16 + b, 8, stride=2)
            part[0, at, :] = low
            part[1, at, :] = high
            part[2, at, :] = pltpu.roll(early, (32 * s + 32) % LANES, 1)
            return carry

        lax.fori_loop(0, 8, tree, 0)

    pl.semaphore_wait(barrier, NT + 2)

    def gather(j, put):
        for pair in range(2):
            starts = [2 * span_ref[j, band * SUBS + 2 * pair + i] + (2 * pair + i) * 64 for i in range(2)]
            for h in range(2):
                both = jnp.concatenate([part[h, pl.ds(starts[i], 8), :] for i in range(2)], axis=0)
                put(h * 32 + pair * 16, both.astype(jnp.bfloat16))
        early = part[2, pl.ds(2 * span_ref[j, band * SUBS], 8), :]
        for s in range(1, SUBS):
            early = early + part[2, pl.ds(2 * span_ref[j, band * SUBS + s] + s * 64, 8), :]
        put(64, jnp.concatenate([early, jnp.zeros_like(early)], axis=0).astype(jnp.bfloat16))

    def outgoing(i):
        return pltpu.make_async_remote_copy(
            src_ref=send.at[i], dst_ref=recv.at[core, me],
            send_sem=send_sem.at[i], recv_sem=recv_sem.at[i],
            device_id={"trial": lax.rem(me + i, NT)}, device_id_type=MESH,
        )

    def forward(i):
        source = lax.rem(me + NT - i, NT)
        return pltpu.make_async_remote_copy(
            src_ref=recv.at[core, source], dst_ref=recv.at[core, source],
            send_sem=fsend_sem.at[i], recv_sem=frecv_sem.at[i],
            device_id={"band": sibling}, device_id_type=MESH,
        )

    def send_out(i, carry):
        def put(row, value):
            send[i, row : row + 16, :] = value

        gather(lax.rem(me + i, NT), put)
        outgoing(i).start()
        return carry

    lax.fori_loop(1, NT, send_out, 0)

    def put_own(row, value):
        recv[core, me, row : row + 16, :] = value

    gather(me, put_own)
    forward(0).start()

    def pass_on(i, carry):
        outgoing(i).wait_recv()
        forward(i).start()
        return carry

    lax.fori_loop(1, NT, pass_on, 0)

    def take(i, carry):
        outgoing(i).wait_send()
        return carry

    lax.fori_loop(1, NT, take, 0)

    def arrived(i, carry):
        forward(i).wait()
        return carry

    lax.fori_loop(0, NT, arrived, 0)

    def spread(block, carry):
        for c in range(2):
            early = recv[c, block + 1, 64:80, :].astype(jnp.float32)[0:8]
            for h in range(2):
                for pair in range(2):
                    both = recv[c, block, h * 32 + pair * 16 : h * 32 + pair * 16 + 16, :].astype(jnp.float32)
                    for i in range(2):
                        s = 2 * pair + i
                        value = both[i * 8 : (i + 1) * 8]
                        if h == 1:
                            moved = pltpu.roll(early, (96 - 32 * s) % LANES, 1) if s != 3 else early
                            value = value + jnp.where(lane >= 96, moved, 0.0)
                        rows[pl.ds((c * SUBS + s) * 8 * PITCH + 2 * block + h, 8, stride=PITCH), :] = value
        return carry

    lax.fori_loop(0, NT, spread, 0)

    lane4 = lax.broadcasted_iota(jnp.int32, (ROWS, LANES), 1)

    def trial_sums(owner, g):
        at = owner * 16 + core * 8 + g
        sums = [jnp.zeros((ROWS, LANES), jnp.float32) for b in range(2)]
        for e in range(8):
            shift = off_ref[at, z * 8 + e]
            fine = jnp.bitwise_and(shift, LANES - 1)
            base = (e * 8 + 2 * rel_ref[at, z * 8 + e]) * PITCH + lax.shift_right_logical(shift, 7)
            turn = jnp.bitwise_and(LANES - fine, LANES - 1)
            for b in range(2):
                here = rows[pl.ds(base + b * PITCH, ROWS), :]
                after = rows[pl.ds(base + b * PITCH + 1, ROWS), :]
                sums[b] = sums[b] + pltpu.roll(jnp.where(lane4 >= fine, here, after), turn, 1)
        return sums

    def far(b):
        return pltpu.make_async_remote_copy(
            src_ref=chunk.at[0, b], dst_ref=relay.at[b],
            send_sem=zsend_sem.at[b], recv_sem=zrecv_sem.at[b],
            device_id={"band": up if b == 0 else down}, device_id_type=MESH,
        )

    def close(side, b):
        return pltpu.make_async_remote_copy(
            src_ref=chunk.at[1 + side, b], dst_ref=near.at[side, b],
            send_sem=zsend_sem.at[2 + 2 * side + b], recv_sem=zrecv_sem.at[2 + 2 * side + b],
            device_id={"band": up if side == 0 else down}, device_id_type=MESH,
        )

    def far_trial(g, carry):
        sums = trial_sums(lax.rem(z + 2, 4), g)
        for b in range(2):
            chunk[0, b, pl.ds(pl.multiple_of(g * ROWS, ROWS), ROWS), :] = sums[b].astype(jnp.bfloat16)
        return carry

    lax.fori_loop(0, 8, far_trial, 0)
    for b in range(2):
        far(b).start()

    for side in range(2):
        def near_trial(g, carry):
            sums = trial_sums(lax.rem(z + 1 + 2 * side, 4), g)
            at = pl.ds(pl.multiple_of(g * ROWS, ROWS), ROWS)
            half[side, at, :] = sums[side]
            chunk[1 + side, 1 - side, at, :] = sums[1 - side].astype(jnp.bfloat16)
            return carry

        lax.fori_loop(0, 8, near_trial, 0)
        close(side, 1 - side).start()

    for side in range(2):
        far(side).wait_recv()
        chunk[1 + side, side] = (half[side] + relay[side].astype(jnp.float32)).astype(jnp.bfloat16)
        close(side, side).start()

    def own_trial(g, carry):
        sums = trial_sums(z, g)
        at = pl.ds(pl.multiple_of(g * ROWS, ROWS), ROWS)
        for b in range(2):
            total[b, at, :] = sums[b]
        return carry

    lax.fori_loop(0, 8, own_trial, 0)

    for b in range(2):
        for side in (b, 1 - b)[::-1]:
            close(side, b).wait_recv()
        total[b] = (
            total[b] + (near[0, b].astype(jnp.float32) + near[1, b].astype(jnp.float32))
        ) * (1.0 / math.sqrt(CH))

    for row in range(ROWS):
        pieces = [total[b, pl.ds(row, 8, stride=ROWS), :] for b in range(2)]
        flat[row * 16 : (row + 1) * 16, :] = jnp.concatenate(pieces, axis=0).astype(jnp.bfloat16)
        for b in range(2):
            series_ref[b, :, row * LANES : (row + 1) * LANES] = pieces[b].astype(jnp.bfloat16)

    best = None
    for part_of in range(4):
        low = part_of * 128
        pair = jnp.concatenate([flat[low : low + 128, :], flat[low + 16 : low + 144, :]], axis=1)
        sums = jnp.dot(pair, window[...], preferred_element_type=jnp.float32)
        for row in range(8):
            piece = sums[row * 16 : (row + 1) * 16]
            best = piece if best is None else jnp.maximum(best, piece)
    for w in range(4):
        top = jnp.max(best[:, w * LANES : (w + 1) * LANES], axis=1, keepdims=True)
        root = jnp.sqrt(jnp.full((16, 1), width_ref[w], jnp.int32).astype(jnp.float32))
        top = top / root
        for b in range(2):
            peaks_ref[b, :, w : w + 1] = top[b * 8 : (b + 1) * 8]

    for b in range(2):
        far(b).wait_send()
        for side in range(2):
            close(side, b).wait_send()


def local(intensity, fine_delay, span_start, sub_rel, offset, widths):
    smem = pl.BlockSpec(memory_space=pltpu.SMEM)
    vmem = pl.BlockSpec(memory_space=pltpu.VMEM)
    hbm = pl.BlockSpec(memory_space=pl.ANY)
    return pl.pallas_call(
        kernel,
        out_shape=(
            jax.ShapeDtypeStruct((2, 8, ROWS * LANES), jnp.bfloat16),
            jax.ShapeDtypeStruct((2, 8, 4), jnp.float32),
        ),
        in_specs=[hbm, hbm, smem, smem, smem, smem],
        out_specs=(vmem, vmem),
        scratch_shapes=[
            pltpu.VMEM((2, SUBS * CSUB, BLOCK), jnp.bfloat16),
            pltpu.VMEM((SUBS, Q, CSUB), jnp.int32),
            pltpu.VMEM((MAXD1 * Q, CSUB), jnp.bfloat16),
            pltpu.VMEM((2, MAXD1 * Q, BLOCK), jnp.float32),
            pltpu.VMEM((3, SUBS * Q * 2, LANES), jnp.float32),
            pltpu.VMEM((NT, MSG, LANES), jnp.bfloat16),
            pltpu.VMEM((2, NT + 1, MSG, LANES), jnp.bfloat16),
            pltpu.VMEM((64 * PITCH, LANES), jnp.float32),
            pltpu.VMEM((2, 8 * ROWS, LANES), jnp.bfloat16),
            pltpu.VMEM((3, 2, 8 * ROWS, LANES), jnp.bfloat16),
            pltpu.VMEM((2, 8 * ROWS, LANES), jnp.float32),
            pltpu.VMEM((2, 2, 8 * ROWS, LANES), jnp.bfloat16),
            pltpu.VMEM((2, 8 * ROWS, LANES), jnp.float32),
            pltpu.VMEM((16 * ROWS + 16, LANES), jnp.bfloat16),
            pltpu.VMEM((2 * LANES, 4 * LANES), jnp.bfloat16),
            pltpu.SemaphoreType.DMA((2, SUBS)),
            pltpu.SemaphoreType.DMA((NT,)),
            pltpu.SemaphoreType.DMA((NT,)),
            pltpu.SemaphoreType.DMA((NT,)),
            pltpu.SemaphoreType.DMA((NT,)),
            pltpu.SemaphoreType.DMA((6,)),
            pltpu.SemaphoreType.DMA((6,)),
        ],
        compiler_params=pltpu.CompilerParams(
            collective_id=0, has_side_effects=True, vmem_limit_bytes=40 * 1024 * 1024
        ),
        name="dedisperse",
    )(intensity, fine_delay, span_start, sub_rel, offset, widths)


def solution(mesh):
    return jax.shard_map(
        local,
        mesh=mesh,
        in_specs=(
            P(None, "band", "trial"),
            P("band", None, None),
            P(),
            P("trial", None),
            P("trial", None),
            P(),
        ),
        out_specs=(P(None, ("trial", "band"), None), P(None, ("trial", "band"), None)),
        check_vma=False,
    )
```

```python
import math

import jax
import jax.numpy as jnp
from jax import lax
from jax.experimental import pallas as pl
from jax.experimental.pallas import tpu as pltpu
from jax.sharding import PartitionSpec as P

CH = 16384
QSPAN = 4
MAXD1 = 32
MAXD2 = 2048
LANES = 128
NT = 16
SUBS = 4
CSUB = 512
Q = 32
BLOCK = 256
ROWS = 32
PITCH = ROWS + MAXD2 // LANES + 1
MSG = 80
MESH = pl.DeviceIdType.MESH


def leaves(level, k):
    if level == 0:
        return [k]
    return leaves(level - 1, k) + leaves(level - 1, k + (MAXD1 >> level))


LEAVES = leaves(5, 0)


def shift_add(first, second, step, lane):
    keep = lane < LANES - step
    low = pltpu.roll(second[1], LANES - step, 1)
    high = pltpu.roll(second[2], LANES - step, 1)
    if second[0] is None:
        early = jnp.where(keep, 0.0, low)
    else:
        early = jnp.where(keep, pltpu.roll(second[0], LANES - step, 1), low)
    if first[0] is not None:
        early = early + first[0]
    return (
        early,
        first[1] + jnp.where(keep, low, high),
        first[2] + jnp.where(keep, high, 0.0),
    )


def kernel(
    x_hbm, delay_hbm, span_hbm, rel_hbm, off_hbm, width_hbm,
    series_ref, peaks_ref,
    xv, dv, span_ref, rel_ref, off_ref, width_ref, lag, part, send, recv, rows, relay, chunk, half, near, total, flat, window,
    in_sem, small_sem, send_sem, recv_sem, fsend_sem, frecv_sem, zsend_sem, zrecv_sem,
):
    band = lax.axis_index("band")
    me = lax.axis_index("trial")
    z = lax.div(band, 2)
    core = lax.rem(band, 2)
    sibling = band + 1 - 2 * core
    up = lax.rem(band + 2, 8)
    down = lax.rem(band + 6, 8)

    barrier = pltpu.get_barrier_semaphore()

    def greet(i, carry):
        pl.semaphore_signal(barrier, inc=1, device_id={"trial": lax.rem(me + i, NT)}, device_id_type=MESH)
        return carry

    lax.fori_loop(1, NT, greet, 0)
    for other in (sibling, up, down):
        pl.semaphore_signal(barrier, inc=1, device_id={"band": other}, device_id_type=MESH)

    def load(s):
        cut = pl.ds(s * CSUB, CSUB)
        return (
            pltpu.make_async_copy(x_hbm.at[:, cut, :], xv.at[:, cut, :], in_sem.at[0, s]),
            pltpu.make_async_copy(delay_hbm.at[s], dv.at[s], in_sem.at[1, s]),
        )

    for s in range(SUBS):
        for copy in load(s):
            copy.start()

    own_bands = pl.ds(pl.multiple_of(z * 8, 8), 8)
    small = [
        pltpu.make_async_copy(span_hbm, span_ref, small_sem.at[0]),
        pltpu.make_async_copy(rel_hbm.at[own_bands, :], rel_ref, small_sem.at[1]),
        pltpu.make_async_copy(off_hbm.at[own_bands, :], off_ref, small_sem.at[2]),
        pltpu.make_async_copy(width_hbm, width_ref, small_sem.at[3]),
    ]
    for copy in small:
        copy.start()

    lane = lax.broadcasted_iota(jnp.int32, (8, LANES), 1)
    rows[...] = jnp.zeros_like(rows)
    recv[0, NT] = jnp.zeros_like(recv[0, NT])
    recv[1, NT] = jnp.zeros_like(recv[1, NT])
    flat[...] = jnp.zeros_like(flat)

    group = lax.broadcasted_iota(jnp.int32, (8, LANES), 1) // Q
    lag[:, :, 0:8, :] = jnp.zeros((8, 2, 8, LANES), jnp.float32)
    lag[:, :, 8 + BLOCK :, :] = jnp.zeros((8, 2, 8, LANES), jnp.float32)
    one = jnp.ones((), jnp.bfloat16)
    zero = jnp.zeros((), jnp.bfloat16)
    for s in range(SUBS):
        for copy in load(s):
            copy.wait()
        times = jnp.concatenate(
            [xv[b, s * CSUB : (s + 1) * CSUB, :].T for b in range(2)], axis=0
        )
        delays = dv[s].astype(jnp.float32)
        delays = jnp.concatenate([delays - 8.0 * j for j in range(4)], axis=0).T.astype(jnp.bfloat16)
        for m in range(0, 8, 2):
            sel = jnp.concatenate(
                [jnp.where(delays == jnp.bfloat16(m + i), one, zero) for i in range(2)], axis=1
            )
            product = jnp.dot(times, sel, preferred_element_type=jnp.float32)
            for i in range(2):
                for b in range(2):
                    lag[m + i, b, 8 : 8 + BLOCK, :] = product[
                        b * BLOCK : (b + 1) * BLOCK, i * LANES : (i + 1) * LANES
                    ]
        for b in range(2):
            sums = []
            for v in range(BLOCK // 8 + 1):
                add = lag[0, b, 8 * v : 8 * v + 8, :]
                for m in range(1, 8):
                    add = add + lag[m, b, 8 * v + m : 8 * v + m + 8, :]
                sums.append(add)

            def at(v):
                return sums[v] if 0 <= v < len(sums) else jnp.zeros((8, LANES), jnp.float32)

            lined = []
            for v in range(-3, BLOCK // 8 + 1):
                line = at(v)
                for j in range(1, 4):
                    line = jnp.where(group == j, at(v + j), line)
                lined.append(line)
            lined = [jnp.zeros((8, LANES), jnp.float32)] * 12 + lined
            for tile in range(3):
                turned = jnp.concatenate(lined[16 * tile : 16 * tile + 16], axis=0).T
                folded = (turned[0:32] + turned[32:64]) + (turned[64:96] + turned[96:128])
                part[(tile + 2) % 3, pl.ds(s * 64 + b, 32, stride=2), :] = folded

    for copy in small:
        copy.wait()
    pl.semaphore_wait(barrier, NT + 2)

    def gather(j, put):
        for pair in range(2):
            starts = [2 * span_ref[j, band * SUBS + 2 * pair + i] + (2 * pair + i) * 64 for i in range(2)]
            for h in range(2):
                both = jnp.concatenate([part[h, pl.ds(starts[i], 8), :] for i in range(2)], axis=0)
                put(h * 32 + pair * 16, both.astype(jnp.bfloat16))
        early = part[2, pl.ds(2 * span_ref[j, band * SUBS + 3] + 192, 8), :]
        for s in range(3):
            more = part[2, pl.ds(2 * span_ref[j, band * SUBS + s] + s * 64, 8), :]
            early = early + pltpu.roll(more, 32 * s + 32, 1)
        put(64, jnp.concatenate([early, jnp.zeros_like(early)], axis=0).astype(jnp.bfloat16))

    def outgoing(i):
        return pltpu.make_async_remote_copy(
            src_ref=send.at[i], dst_ref=recv.at[core, me],
            send_sem=send_sem.at[i], recv_sem=recv_sem.at[i],
            device_id={"trial": lax.rem(me + i, NT)}, device_id_type=MESH,
        )

    def forward(i):
        source = lax.rem(me + NT - i, NT)
        return pltpu.make_async_remote_copy(
            src_ref=recv.at[core, source], dst_ref=recv.at[core, source],
            send_sem=fsend_sem.at[i], recv_sem=frecv_sem.at[i],
            device_id={"band": sibling}, device_id_type=MESH,
        )

    def send_out(i, carry):
        def put(row, value):
            send[i, row : row + 16, :] = value

        gather(lax.rem(me + i, NT), put)
        outgoing(i).start()
        return carry

    lax.fori_loop(1, NT, send_out, 0)

    def put_own(row, value):
        recv[core, me, row : row + 16, :] = value

    gather(me, put_own)
    forward(0).start()

    ahead = lax.broadcasted_iota(jnp.int32, (2 * LANES, LANES), 0) - lax.broadcasted_iota(
        jnp.int32, (2 * LANES, LANES), 1
    )
    for w in range(4):
        inside = (ahead >= 0) & (ahead < width_ref[w])
        window[:, w * LANES : (w + 1) * LANES] = jnp.where(inside, 1.0, 0.0).astype(jnp.bfloat16)

    def pass_on(i, carry):
        outgoing(i).wait_recv()
        forward(i).start()
        return carry

    lax.fori_loop(1, NT, pass_on, 0)

    def take(i, carry):
        outgoing(i).wait_send()
        return carry

    lax.fori_loop(1, NT, take, 0)

    def arrived(i, carry):
        forward(i).wait()
        return carry

    lax.fori_loop(0, NT, arrived, 0)

    def spread(block, carry):
        for c in range(2):
            early = recv[c, block + 1, 64:80, :].astype(jnp.float32)[0:8]
            for h in range(2):
                for pair in range(2):
                    both = recv[c, block, h * 32 + pair * 16 : h * 32 + pair * 16 + 16, :].astype(jnp.float32)
                    for i in range(2):
                        s = 2 * pair + i
                        value = both[i * 8 : (i + 1) * 8]
                        if h == 1:
                            moved = pltpu.roll(early, (96 - 32 * s) % LANES, 1) if s != 3 else early
                            value = value + jnp.where(lane >= 96, moved, 0.0)
                        rows[pl.ds((c * SUBS + s) * 8 * PITCH + 2 * block + h, 8, stride=PITCH), :] = value
        return carry

    lax.fori_loop(0, NT, spread, 0)

    lane4 = lax.broadcasted_iota(jnp.int32, (ROWS, LANES), 1)

    def trial_sums(owner, g):
        at = owner * 16 + core * 8 + g
        sums = [jnp.zeros((ROWS, LANES), jnp.float32) for b in range(2)]
        for e in range(8):
            shift = off_ref[e, at]
            fine = jnp.bitwise_and(shift, LANES - 1)
            base = (e * 8 + 2 * rel_ref[e, at]) * PITCH + lax.shift_right_logical(shift, 7)
            turn = jnp.bitwise_and(LANES - fine, LANES - 1)
            for b in range(2):
                here = rows[pl.ds(base + b * PITCH, ROWS), :]
                after = rows[pl.ds(base + b * PITCH + 1, ROWS), :]
                sums[b] = sums[b] + pltpu.roll(jnp.where(lane4 >= fine, here, after), turn, 1)
        return sums

    def far(b):
        return pltpu.make_async_remote_copy(
            src_ref=chunk.at[0, b], dst_ref=relay.at[b],
            send_sem=zsend_sem.at[b], recv_sem=zrecv_sem.at[b],
            device_id={"band": up if b == 0 else down}, device_id_type=MESH,
        )

    def close(side, b):
        return pltpu.make_async_remote_copy(
            src_ref=chunk.at[1 + side, b], dst_ref=near.at[side, b],
            send_sem=zsend_sem.at[2 + 2 * side + b], recv_sem=zrecv_sem.at[2 + 2 * side + b],
            device_id={"band": up if side == 0 else down}, device_id_type=MESH,
        )

    def far_trial(g, carry):
        sums = trial_sums(lax.rem(z + 2, 4), g)
        for b in range(2):
            chunk[0, b, pl.ds(pl.multiple_of(g * ROWS, ROWS), ROWS), :] = sums[b].astype(jnp.bfloat16)
        return carry

    lax.fori_loop(0, 8, far_trial, 0)
    for b in range(2):
        far(b).start()

    for side in range(2):
        def near_trial(g, carry):
            sums = trial_sums(lax.rem(z + 1 + 2 * side, 4), g)
            at = pl.ds(pl.multiple_of(g * ROWS, ROWS), ROWS)
            half[side, at, :] = sums[side]
            chunk[1 + side, 1 - side, at, :] = sums[1 - side].astype(jnp.bfloat16)
            return carry

        lax.fori_loop(0, 8, near_trial, 0)
        close(side, 1 - side).start()

    for side in range(2):
        far(side).wait_recv()
        chunk[1 + side, side] = (half[side] + relay[side].astype(jnp.float32)).astype(jnp.bfloat16)
        close(side, side).start()

    def own_trial(g, carry):
        sums = trial_sums(z, g)
        at = pl.ds(pl.multiple_of(g * ROWS, ROWS), ROWS)
        for b in range(2):
            total[b, at, :] = sums[b]
        return carry

    lax.fori_loop(0, 8, own_trial, 0)

    for b in range(2):
        for side in (b, 1 - b)[::-1]:
            close(side, b).wait_recv()
        total[b] = (
            total[b] + (near[0, b].astype(jnp.float32) + near[1, b].astype(jnp.float32))
        ) * (1.0 / math.sqrt(CH))

    for row in range(ROWS):
        pieces = [total[b, pl.ds(row, 8, stride=ROWS), :] for b in range(2)]
        flat[row * 16 : (row + 1) * 16, :] = jnp.concatenate(pieces, axis=0).astype(jnp.bfloat16)
        for b in range(2):
            series_ref[b, :, row * LANES : (row + 1) * LANES] = pieces[b].astype(jnp.bfloat16)

    best = None
    for part_of in range(4):
        low = part_of * 128
        pair = jnp.concatenate([flat[low : low + 128, :], flat[low + 16 : low + 144, :]], axis=1)
        sums = jnp.dot(pair, window[...], preferred_element_type=jnp.float32)
        for row in range(8):
            piece = sums[row * 16 : (row + 1) * 16]
            best = piece if best is None else jnp.maximum(best, piece)
    for w in range(4):
        top = jnp.max(best[:, w * LANES : (w + 1) * LANES], axis=1, keepdims=True)
        root = jnp.sqrt(jnp.full((16, 1), width_ref[w], jnp.int32).astype(jnp.float32))
        top = top / root
        for b in range(2):
            peaks_ref[b, :, w : w + 1] = top[b * 8 : (b + 1) * 8]

    for b in range(2):
        far(b).wait_send()
        for side in range(2):
            close(side, b).wait_send()


def local(intensity, fine_delay, span_start, sub_rel, offset, widths):
    vmem = pl.BlockSpec(memory_space=pltpu.VMEM)
    hbm = pl.BlockSpec(memory_space=pltpu.HBM)
    return pl.pallas_call(
        kernel,
        out_shape=(
            jax.ShapeDtypeStruct((2, 8, ROWS * LANES), jnp.bfloat16),
            jax.ShapeDtypeStruct((2, 8, 4), jnp.float32),
        ),
        in_specs=[hbm] * 6,
        out_specs=(vmem, vmem),
        scratch_shapes=[
            pltpu.VMEM((2, SUBS * CSUB, BLOCK), jnp.bfloat16),
            pltpu.VMEM((SUBS, Q, CSUB), jnp.int32),
            pltpu.SMEM((NT, 32), jnp.int32),
            pltpu.SMEM((8, 64), jnp.int32),
            pltpu.SMEM((8, 64), jnp.int32),
            pltpu.SMEM((4,), jnp.int32),
            pltpu.VMEM((8, 2, BLOCK + 16, LANES), jnp.float32),
            pltpu.VMEM((3, SUBS * Q * 2, LANES), jnp.float32),
            pltpu.VMEM((NT, MSG, LANES), jnp.bfloat16),
            pltpu.VMEM((2, NT + 1, MSG, LANES), jnp.bfloat16),
            pltpu.VMEM((64 * PITCH, LANES), jnp.float32),
            pltpu.VMEM((2, 8 * ROWS, LANES), jnp.bfloat16),
            pltpu.VMEM((3, 2, 8 * ROWS, LANES), jnp.bfloat16),
            pltpu.VMEM((2, 8 * ROWS, LANES), jnp.float32),
            pltpu.VMEM((2, 2, 8 * ROWS, LANES), jnp.bfloat16),
            pltpu.VMEM((2, 8 * ROWS, LANES), jnp.float32),
            pltpu.VMEM((16 * ROWS + 16, LANES), jnp.bfloat16),
            pltpu.VMEM((2 * LANES, 4 * LANES), jnp.bfloat16),
            pltpu.SemaphoreType.DMA((2, SUBS)),
            pltpu.SemaphoreType.DMA((4,)),
            pltpu.SemaphoreType.DMA((NT,)),
            pltpu.SemaphoreType.DMA((NT,)),
            pltpu.SemaphoreType.DMA((NT,)),
            pltpu.SemaphoreType.DMA((NT,)),
            pltpu.SemaphoreType.DMA((6,)),
            pltpu.SemaphoreType.DMA((6,)),
        ],
        compiler_params=pltpu.CompilerParams(
            collective_id=0, has_side_effects=True, vmem_limit_bytes=67043328
        ),
        name="dedisperse",
    )(intensity, fine_delay, span_start, sub_rel.T, offset.T, widths)


def solution(mesh):
    return jax.shard_map(
        local,
        mesh=mesh,
        in_specs=(
            P(None, "band", "trial"),
            P("band", None, None),
            P(),
            P("trial", None),
            P("trial", None),
            P(),
        ),
        out_specs=(P(None, ("trial", "band"), None), P(None, ("trial", "band"), None)),
        check_vma=False,
    )
```

```python
import math

import jax
import jax.numpy as jnp
from jax import lax
from jax.experimental import pallas as pl
from jax.experimental.pallas import tpu as pltpu
from jax.sharding import PartitionSpec as P

CH = 16384
QSPAN = 4
MAXD1 = 32
MAXD2 = 2048
LANES = 128
NT = 16
SUBS = 4
CSUB = 512
Q = 32
BLOCK = 256
ROWS = 32
PITCH = ROWS + MAXD2 // LANES + 1
MSG = 80
VMEM_MIB = 32
FAR_FIRST = (10, 9, 11, 6, 14, 8, 2, 5, 7, 13, 15, 12, 4, 1, 3)
MESH = pl.DeviceIdType.MESH


def leaves(level, k):
    if level == 0:
        return [k]
    return leaves(level - 1, k) + leaves(level - 1, k + (MAXD1 >> level))


LEAVES = leaves(5, 0)


def shift_add(first, second, step, lane):
    keep = lane < LANES - step
    low = pltpu.roll(second[1], LANES - step, 1)
    high = pltpu.roll(second[2], LANES - step, 1)
    if second[0] is None:
        early = jnp.where(keep, 0.0, low)
    else:
        early = jnp.where(keep, pltpu.roll(second[0], LANES - step, 1), low)
    if first[0] is not None:
        early = early + first[0]
    return (
        early,
        first[1] + jnp.where(keep, low, high),
        first[2] + jnp.where(keep, high, 0.0),
    )


def kernel(
    x_hbm, delay_hbm, span_hbm, rel_hbm, off_hbm, width_hbm,
    total, near, window, roots,
    xv, dv, span_ref, rel_ref, off_ref, width_ref, lag, part, send, recv, rows, relay, chunk, half, acc,
    in_sem, small_sem, send_sem, recv_sem, fsend_sem, frecv_sem, zsend_sem, zrecv_sem,
):
    band = lax.axis_index("band")
    me = lax.axis_index("trial")
    z = lax.div(band, 2)
    core = lax.rem(band, 2)
    sibling = band + 1 - 2 * core
    up = lax.rem(band + 2, 8)
    down = lax.rem(band + 6, 8)

    barrier = pltpu.get_barrier_semaphore()

    def load(s):
        cut = pl.ds(s * CSUB, CSUB)
        return (
            pltpu.make_async_copy(x_hbm.at[:, cut, :], xv.at[:, cut, :], in_sem.at[0, s]),
            pltpu.make_async_copy(delay_hbm.at[s], dv.at[s], in_sem.at[1, s]),
        )

    for s in range(SUBS):
        for copy in load(s):
            copy.start()

    def greet(i, carry):
        pl.semaphore_signal(barrier, inc=1, device_id={"trial": lax.rem(me + i, NT)}, device_id_type=MESH)
        return carry

    lax.fori_loop(1, NT, greet, 0)
    for other in (sibling, up, down):
        pl.semaphore_signal(barrier, inc=1, device_id={"band": other}, device_id_type=MESH)

    own_bands = pl.ds(pl.multiple_of(z * 8, 8), 8)
    small = [
        pltpu.make_async_copy(span_hbm, span_ref, small_sem.at[0]),
        pltpu.make_async_copy(rel_hbm.at[own_bands, :], rel_ref, small_sem.at[1]),
        pltpu.make_async_copy(off_hbm.at[own_bands, :], off_ref, small_sem.at[2]),
        pltpu.make_async_copy(width_hbm, width_ref, small_sem.at[3]),
    ]
    for copy in small:
        copy.start()

    lane = lax.broadcasted_iota(jnp.int32, (8, LANES), 1)
    rows[...] = jnp.zeros_like(rows)
    recv[0, NT] = jnp.zeros_like(recv[0, NT])
    recv[1, NT] = jnp.zeros_like(recv[1, NT])

    def gather(pair, j, put):
        starts = [2 * span_ref[j, band * SUBS + 2 * pair + i] + (2 * pair + i) * 64 for i in range(2)]
        for h in range(2):
            both = [part[h, pl.ds(start, 8), :] for start in starts]
            put(pair * 40 + h * 16, jnp.concatenate(both, axis=0).astype(jnp.bfloat16))
        early = [part[2, pl.ds(start, 8), :] for start in starts]
        put(pair * 40 + 32, (pltpu.roll(early[0], 96, 1) + early[1]).astype(jnp.bfloat16))

    def outgoing(pair, i):
        cut = pl.ds(pair * 40, 40)
        return pltpu.make_async_remote_copy(
            src_ref=send.at[i, cut, :], dst_ref=recv.at[core, me, cut, :],
            send_sem=send_sem.at[pair, i], recv_sem=recv_sem.at[pair, i],
            device_id={"trial": lax.rem(me + i, NT)}, device_id_type=MESH,
        )

    def send_pair(pair):
        for i in FAR_FIRST:

            def put(row, value):
                send[i, row : row + value.shape[0], :] = value

            gather(pair, lax.rem(me + i, NT), put)
            outgoing(pair, i).start()

        def put_own(row, value):
            recv[core, me, row : row + value.shape[0], :] = value

        gather(pair, me, put_own)

    group = lax.broadcasted_iota(jnp.int32, (8, LANES), 1) // Q
    blank = jnp.zeros((8, LANES), jnp.float32)
    lag[:, :, :, 0:8, :] = jnp.zeros((2, 8, 2, 8, LANES), jnp.float32)
    lag[:, :, :, 8 + BLOCK :, :] = jnp.zeros((2, 8, 2, 8, LANES), jnp.float32)
    one = jnp.ones((), jnp.bfloat16)
    zero = jnp.zeros((), jnp.bfloat16)

    times, lagged = {}, {}

    def turn_data(s, b):
        times[s, b] = xv[b, s * CSUB : (s + 1) * CSUB, :].T

    def turn_delays(s):
        delays = dv[s].astype(jnp.float32)
        delays = jnp.concatenate([delays - 8.0 * j for j in range(4)], axis=0)
        lagged[s] = delays.T.astype(jnp.bfloat16)

    def product(s, m):
        delays = lagged[s]
        sel = jnp.concatenate(
            [jnp.where(delays == jnp.bfloat16(m + i), one, zero) for i in range(2)], axis=1
        )
        result = jnp.dot(jnp.concatenate([times[s, 0], times[s, 1]], axis=0), sel, preferred_element_type=jnp.float32)
        for i in range(2):
            for b in range(2):
                lag[s % 2, m + i, b, 8 : 8 + BLOCK, :] = result[
                    b * BLOCK : (b + 1) * BLOCK, i * LANES : (i + 1) * LANES
                ]

    def fold(s, b):
        sums = {}

        def at(v):
            if not 0 <= v <= BLOCK // 8:
                return blank
            if v not in sums:
                add = lag[s % 2, 0, b, 8 * v : 8 * v + 8, :]
                for m in range(1, 8):
                    add = add + lag[s % 2, m, b, 8 * v + m : 8 * v + m + 8, :]
                sums[v] = add
            return sums[v]

        def line(v):
            if v < -3:
                return blank
            picked = at(v)
            for j in range(1, 4):
                picked = jnp.where(group == j, at(v + j), picked)
            return picked

        for tile in range(3):
            turned = jnp.concatenate([line(16 * tile - 15 + i) for i in range(16)], axis=0).T
            folded = (turned[0:32] + turned[32:64]) + (turned[64:96] + turned[96:128])
            part[(tile + 2) % 3, pl.ds(s * 64 + b, 32, stride=2), :] = folded

    def arrive(s):
        for copy in load(s):
            copy.wait()

    arrive(0)
    turn_data(0, 0)
    turn_data(0, 1)
    turn_delays(0)
    for s in range(SUBS):
        if s + 1 < SUBS:
            arrive(s + 1)
        product(s, 0)
        if s % 2 == 1:
            fold(s - 1, 0)
        product(s, 2)
        if s + 1 < SUBS:
            turn_data(s + 1, 0)
        product(s, 4)
        if s % 2 == 1:
            fold(s - 1, 1)
        product(s, 6)
        if s + 1 < SUBS:
            turn_data(s + 1, 1)
            turn_delays(s + 1)
        if s % 2 == 1:
            fold(s, 0)
            fold(s, 1)
            if s == 1:
                for copy in small:
                    copy.wait()
                pl.semaphore_wait(barrier, NT + 2)
            send_pair(s // 2)

    def forward(pair):
        cut = (core, pl.ds(0, NT), pl.ds(pair * 40, 40))
        return pltpu.make_async_remote_copy(
            src_ref=recv.at[cut], dst_ref=recv.at[cut],
            send_sem=fsend_sem.at[pair], recv_sem=frecv_sem.at[pair],
            device_id={"band": sibling}, device_id_type=MESH,
        )

    def collect(pair):
        def wait_one(i, carry):
            outgoing(pair, i).wait_recv()
            return carry

        lax.fori_loop(1, NT, wait_one, 0)
        forward(pair).start()

    def spread(c, pair):
        def one_block(block, carry):
            early = recv[c, block + 1, pair * 40 + 32 : pair * 40 + 40, :].astype(jnp.float32)
            for h in range(2):
                both = recv[c, block, pair * 40 + h * 16 : pair * 40 + h * 16 + 16, :].astype(jnp.float32)
                for i in range(2):
                    value = both[i * 8 : (i + 1) * 8]
                    if h == 1:
                        moved = pltpu.roll(early, 32, 1) if i == 0 else early
                        value = value + jnp.where(lane >= 96, moved, 0.0)
                    rows[pl.ds((c * SUBS + 2 * pair + i) * 8 * PITCH + 2 * block + h, 8, stride=PITCH), :] = value
            return carry

        lax.fori_loop(0, NT, one_block, 0, unroll=4)

    ahead = lax.broadcasted_iota(jnp.int32, (2 * LANES, LANES), 0) - lax.broadcasted_iota(
        jnp.int32, (2 * LANES, LANES), 1
    )
    for w in range(4):
        inside = (ahead >= 0) & (ahead < width_ref[w])
        window[:, w * LANES : (w + 1) * LANES] = jnp.where(inside, 1.0, 0.0).astype(jnp.bfloat16)
        root = jnp.sqrt(jnp.full((8, LANES), width_ref[w], jnp.int32).astype(jnp.float32))
        roots[:, w * LANES : (w + 1) * LANES] = root

    lane8 = lax.broadcasted_iota(jnp.int32, (2 * ROWS, LANES), 1)

    def trial_sums(owner, g, subs):
        at = owner * 16 + core * 8 + g
        sums = None
        for e in subs:
            shift = off_ref[e, at]
            fine = jnp.bitwise_and(shift, LANES - 1)
            base = (e * 8 + 2 * rel_ref[e, at]) * PITCH + lax.shift_right_logical(shift, 7)
            turn = jnp.bitwise_and(LANES - fine, LANES - 1)
            here, after = [
                jnp.concatenate([rows[pl.ds(base + b * PITCH + next_row, ROWS), :] for b in range(2)], axis=0)
                for next_row in range(2)
            ]
            joined = jnp.where(lane8 >= fine, here, after).astype(jnp.bfloat16)
            moved = pltpu.roll(joined, turn, 1).astype(jnp.float32)
            sums = moved if sums is None else sums + moved
        return sums

    def piece(b, p):
        return {"band": up if b == 0 else down}, pl.ds(p * 4 * ROWS, 4 * ROWS)

    def far(b, p):
        where, cut = piece(b, p)
        return pltpu.make_async_remote_copy(
            src_ref=chunk.at[0, b, cut, :], dst_ref=relay.at[b, cut, :],
            send_sem=zsend_sem.at[2 * b + p], recv_sem=zrecv_sem.at[2 * b + p],
            device_id=where, device_id_type=MESH,
        )

    def close(side, p):
        where, cut = piece(side, p)
        return pltpu.make_async_remote_copy(
            src_ref=chunk.at[1 + side, side, cut, :], dst_ref=near.at[side, side, cut, :],
            send_sem=zsend_sem.at[4 + 2 * side + p], recv_sem=zrecv_sem.at[4 + 2 * side + p],
            device_id=where, device_id_type=MESH,
        )

    def direct(side):
        return pltpu.make_async_remote_copy(
            src_ref=chunk.at[1 + side, 1 - side], dst_ref=near.at[side, 1 - side],
            send_sem=zsend_sem.at[8 + side], recv_sem=zrecv_sem.at[8 + side],
            device_id={"band": up if side == 0 else down}, device_id_type=MESH,
        )

    def each(g):
        return slice(g * 2 * ROWS, (g + 1) * 2 * ROWS)

    def accumulate(subs, fresh):
        def one_owner(ahead, carry):
            owner = lax.rem(z + ahead, 4)
            for g in range(8):
                sums = trial_sums(owner, g, subs)
                if fresh:
                    acc[ahead, each(g), :] = sums
                else:
                    acc[ahead, each(g), :] += sums
            return carry

        lax.fori_loop(0, 4, one_owner, 0)

    def last(ahead, g):
        other = (1 - core) * SUBS
        sums = acc[ahead, each(g), :] + trial_sums(lax.rem(z + ahead, 4), g, (other + 2, other + 3))
        return sums[:ROWS], sums[ROWS:]

    def line_of(g):
        return slice(g * ROWS, (g + 1) * ROWS)

    collect(0)
    spread(core, 0)
    forward(0).wait()
    spread(1 - core, 0)
    accumulate((0, 1, 4, 5), True)
    collect(1)
    spread(core, 1)
    accumulate((core * SUBS + 2, core * SUBS + 3), False)
    forward(1).wait()
    spread(1 - core, 1)

    for p in range(2):
        for g in range(4 * p, 4 * p + 4):
            sums = last(2, g)
            for b in range(2):
                chunk[0, b, line_of(g), :] = sums[b].astype(jnp.bfloat16)
        for b in range(2):
            far(b, p).start()

    for side in range(2):
        for g in range(8):
            sums = last(1 + 2 * side, g)
            half[side, line_of(g), :] = sums[side]
            chunk[1 + side, 1 - side, line_of(g), :] = sums[1 - side].astype(jnp.bfloat16)
        direct(side).start()

    for g in range(8):
        sums = last(0, g)
        for b in range(2):
            total[b, line_of(g), :] = sums[b]

    for p in range(2):
        cut = slice(p * 4 * ROWS, (p + 1) * 4 * ROWS)
        for side in range(2):
            far(side, p).wait_recv()
            joined = half[side, cut, :] + relay[side, cut, :].astype(jnp.float32)
            chunk[1 + side, side, cut, :] = joined.astype(jnp.bfloat16)
            close(side, p).start()

    def sent(i, carry):
        outgoing(0, i).wait_send()
        outgoing(1, i).wait_send()
        return carry

    lax.fori_loop(1, NT, sent, 0)

    for side in range(2):
        direct(side).wait()
        for p in range(2):
            far(side, p).wait_send()
            close(side, p).wait()


def finish(total, near, window, roots, series_ref, peaks_ref, summed, flat):
    for b in range(2):
        summed[b] = (
            total[b] + (near[0, b].astype(jnp.float32) + near[1, b].astype(jnp.float32))
        ) * (1.0 / math.sqrt(CH))
    flat[16 * ROWS :, :] = jnp.zeros((16, LANES), jnp.bfloat16)

    for row in range(ROWS):
        pieces = [summed[b, pl.ds(row, 8, stride=ROWS), :] for b in range(2)]
        flat[row * 16 : (row + 1) * 16, :] = jnp.concatenate(pieces, axis=0).astype(jnp.bfloat16)
        for b in range(2):
            series_ref[b, :, row * LANES : (row + 1) * LANES] = pieces[b].astype(jnp.bfloat16)

    best = None
    for part_of in range(4):
        low = part_of * 128
        pair = jnp.concatenate([flat[low : low + 128, :], flat[low + 16 : low + 144, :]], axis=1)
        sums = jnp.dot(pair, window[...], preferred_element_type=jnp.float32)
        for row in range(8):
            piece = sums[row * 16 : (row + 1) * 16]
            best = piece if best is None else jnp.maximum(best, piece)
    for w in range(4):
        cut = slice(w * LANES, (w + 1) * LANES)
        top = jnp.max(best[:, cut].T, axis=0, keepdims=True) / roots[0:1, w * LANES : w * LANES + 16]
        for b in range(2):
            peaks_ref[b, w : w + 1, :] = top[:, b * 8 : (b + 1) * 8]


def local(intensity, fine_delay, span_start, sub_rel, offset, widths):
    vmem = pl.BlockSpec(memory_space=pltpu.VMEM)
    hbm = pl.BlockSpec(memory_space=pltpu.HBM)
    pieces = pl.pallas_call(
        kernel,
        out_shape=(
            jax.ShapeDtypeStruct((2, 8 * ROWS, LANES), jnp.float32),
            jax.ShapeDtypeStruct((2, 2, 8 * ROWS, LANES), jnp.bfloat16),
            jax.ShapeDtypeStruct((2 * LANES, 4 * LANES), jnp.bfloat16),
            jax.ShapeDtypeStruct((8, 4 * LANES), jnp.float32),
        ),
        in_specs=[hbm] * 6,
        out_specs=(vmem,) * 4,
        scratch_shapes=[
            pltpu.VMEM((2, SUBS * CSUB, BLOCK), jnp.bfloat16),
            pltpu.VMEM((SUBS, Q, CSUB), jnp.int32),
            pltpu.SMEM((NT, 32), jnp.int32),
            pltpu.SMEM((8, 64), jnp.int32),
            pltpu.SMEM((8, 64), jnp.int32),
            pltpu.SMEM((4,), jnp.int32),
            pltpu.VMEM((2, 8, 2, BLOCK + 16, LANES), jnp.float32),
            pltpu.VMEM((3, SUBS * Q * 2, LANES), jnp.float32),
            pltpu.VMEM((NT, MSG, LANES), jnp.bfloat16),
            pltpu.VMEM((2, NT + 1, MSG, LANES), jnp.bfloat16),
            pltpu.VMEM((64 * PITCH, LANES), jnp.float32),
            pltpu.VMEM((2, 8 * ROWS, LANES), jnp.bfloat16),
            pltpu.VMEM((3, 2, 8 * ROWS, LANES), jnp.bfloat16),
            pltpu.VMEM((2, 8 * ROWS, LANES), jnp.float32),
            pltpu.VMEM((4, 16 * ROWS, LANES), jnp.float32),
            pltpu.SemaphoreType.DMA((2, SUBS)),
            pltpu.SemaphoreType.DMA((4,)),
            pltpu.SemaphoreType.DMA((2, NT)),
            pltpu.SemaphoreType.DMA((2, NT)),
            pltpu.SemaphoreType.DMA((2,)),
            pltpu.SemaphoreType.DMA((2,)),
            pltpu.SemaphoreType.DMA((10,)),
            pltpu.SemaphoreType.DMA((10,)),
        ],
        compiler_params=pltpu.CompilerParams(
            collective_id=0, has_side_effects=True, vmem_limit_bytes=VMEM_MIB * 1024 * 1024
        ),
        name="dedisperse",
    )(*[
        pltpu.with_memory_space_constraint(a, pltpu.HBM)
        for a in (intensity, fine_delay, span_start, sub_rel.T, offset.T, widths)
    ])
    series, peaks = pl.pallas_call(
        finish,
        out_shape=(
            jax.ShapeDtypeStruct((2, 8, ROWS * LANES), jnp.bfloat16),
            jax.ShapeDtypeStruct((2, 4, 8), jnp.float32),
        ),
        in_specs=[vmem] * 4,
        out_specs=(vmem, vmem),
        scratch_shapes=[
            pltpu.VMEM((2, 8 * ROWS, LANES), jnp.float32),
            pltpu.VMEM((16 * ROWS + 16, LANES), jnp.bfloat16),
        ],
        compiler_params=pltpu.CompilerParams(vmem_limit_bytes=VMEM_MIB * 1024 * 1024),
        name="finish",
    )(*pieces)
    return series, peaks.transpose(0, 2, 1)


def solution(mesh):
    return jax.shard_map(
        local,
        mesh=mesh,
        in_specs=(
            P(None, "band", "trial"),
            P("band", None, None),
            P(),
            P("trial", None),
            P("trial", None),
            P(),
        ),
        out_specs=(P(None, ("trial", "band"), None), P(None, ("trial", "band"), None)),
        check_vma=False,
    )
```

```python
import math

import jax
import jax.numpy as jnp
from jax import lax
from jax.experimental import pallas as pl
from jax.experimental.pallas import tpu as pltpu
from jax.sharding import PartitionSpec as P

CH = 16384
QSPAN = 4
MAXD1 = 32
MAXD2 = 2048
LANES = 128
NT = 16
SUBS = 4
CSUB = 512
Q = 32
BLOCK = 256
ROWS = 32
PITCH = ROWS + MAXD2 // LANES + 1
MSG = 80
VMEM_MIB = 32
FAR_FIRST = (10, 9, 11, 6, 14, 8, 2, 5, 7, 13, 15, 12, 4, 1, 3)
MESH = pl.DeviceIdType.MESH


def leaves(level, k):
    if level == 0:
        return [k]
    return leaves(level - 1, k) + leaves(level - 1, k + (MAXD1 >> level))


LEAVES = leaves(5, 0)


def shift_add(first, second, step, lane):
    keep = lane < LANES - step
    low = pltpu.roll(second[1], LANES - step, 1)
    high = pltpu.roll(second[2], LANES - step, 1)
    if second[0] is None:
        early = jnp.where(keep, 0.0, low)
    else:
        early = jnp.where(keep, pltpu.roll(second[0], LANES - step, 1), low)
    if first[0] is not None:
        early = early + first[0]
    return (
        early,
        first[1] + jnp.where(keep, low, high),
        first[2] + jnp.where(keep, high, 0.0),
    )


def kernel(
    x_hbm, delay_hbm, span_hbm, rel_hbm, off_hbm, width_hbm,
    total, near, window, roots,
    xv, dv, span_ref, rel_ref, off_ref, width_ref, lag, part, send, recv, rows, relay, chunk, half, acc,
    in_sem, small_sem, send_sem, recv_sem, fsend_sem, frecv_sem, zsend_sem, zrecv_sem,
):
    band = lax.axis_index("band")
    me = lax.axis_index("trial")
    z = lax.div(band, 2)
    core = lax.rem(band, 2)
    sibling = band + 1 - 2 * core
    up = lax.rem(band + 2, 8)
    down = lax.rem(band + 6, 8)

    barrier = pltpu.get_barrier_semaphore()

    def load(s):
        cut = pl.ds(s * CSUB, CSUB)
        return pltpu.make_async_copy(x_hbm.at[:, cut, :], xv.at[:, cut, :], in_sem.at[s])

    delay_copy = pltpu.make_async_copy(delay_hbm, dv, in_sem.at[SUBS])
    load(0).start()
    delay_copy.start()
    for s in range(1, SUBS):
        load(s).start()

    def greet(i, carry):
        pl.semaphore_signal(barrier, inc=1, device_id={"trial": lax.rem(me + i, NT)}, device_id_type=MESH)
        return carry

    lax.fori_loop(1, NT, greet, 0)
    for other in (sibling, up, down):
        pl.semaphore_signal(barrier, inc=1, device_id={"band": other}, device_id_type=MESH)

    own_bands = pl.ds(pl.multiple_of(z * 8, 8), 8)
    small = [
        pltpu.make_async_copy(span_hbm, span_ref, small_sem.at[0]),
        pltpu.make_async_copy(rel_hbm.at[own_bands, :], rel_ref, small_sem.at[1]),
        pltpu.make_async_copy(off_hbm.at[own_bands, :], off_ref, small_sem.at[2]),
        pltpu.make_async_copy(width_hbm, width_ref, small_sem.at[3]),
    ]
    for copy in small:
        copy.start()

    lane = lax.broadcasted_iota(jnp.int32, (8, LANES), 1)
    rows[...] = jnp.zeros_like(rows)
    recv[0, NT] = jnp.zeros_like(recv[0, NT])
    recv[1, NT] = jnp.zeros_like(recv[1, NT])

    def gather(pair, j, put):
        starts = [2 * span_ref[j, band * SUBS + 2 * pair + i] + (2 * pair + i) * 64 for i in range(2)]
        for h in range(2):
            both = [part[h, pl.ds(start, 8), :] for start in starts]
            put(pair * 40 + h * 16, jnp.concatenate(both, axis=0).astype(jnp.bfloat16))
        early = [part[2, pl.ds(start, 8), :] for start in starts]
        put(pair * 40 + 32, (early[0] + early[1]).astype(jnp.bfloat16))

    def outgoing(pair, i):
        cut = pl.ds(pair * 40, 40)
        return pltpu.make_async_remote_copy(
            src_ref=send.at[i, cut, :], dst_ref=recv.at[core, me, cut, :],
            send_sem=send_sem.at[pair], recv_sem=recv_sem.at[pair],
            device_id={"trial": lax.rem(me + i, NT)}, device_id_type=MESH,
        )

    def all_of(pair):
        cut = pl.ds(pair * 40, 40)
        return pltpu.make_async_remote_copy(
            src_ref=send.at[pl.ds(1, NT - 1), cut, :], dst_ref=recv.at[core, pl.ds(0, NT - 1), cut, :],
            send_sem=send_sem.at[pair], recv_sem=recv_sem.at[pair],
            device_id={"trial": lax.rem(me + 1, NT)}, device_id_type=MESH,
        )

    def send_pair(pair):
        for first in range(0, NT - 1, 5):
            for i in FAR_FIRST[first : first + 5]:

                def put(row, value):
                    send[i, row : row + value.shape[0], :] = value

                gather(pair, lax.rem(me + i, NT), put)
            for i in FAR_FIRST[first : first + 5]:
                outgoing(pair, i).start()

        def put_own(row, value):
            recv[core, me, row : row + value.shape[0], :] = value

        gather(pair, me, put_own)

    group = lax.broadcasted_iota(jnp.int32, (8, LANES), 1) // Q
    blank = jnp.zeros((8, LANES), jnp.float32)
    lag[:, :, :, 0:8, :] = jnp.zeros((2, 8, 2, 8, LANES), jnp.float32)
    lag[:, :, :, 8 + BLOCK :, :] = jnp.zeros((2, 8, 2, 8, LANES), jnp.float32)
    one = jnp.ones((), jnp.bfloat16)
    zero = jnp.zeros((), jnp.bfloat16)

    times, lagged = {}, {}

    def turn_data(s, b):
        times[s, b] = xv[b, s * CSUB : (s + 1) * CSUB, :].T

    def turn_delays(s):
        delays = dv[s].astype(jnp.float32)
        delays = jnp.concatenate([delays - 8.0 * j for j in range(4)], axis=0)
        lagged[s] = delays.astype(jnp.bfloat16).T

    def product(s, m):
        delays = lagged[s]
        sel = jnp.concatenate(
            [jnp.where(delays == jnp.bfloat16(m + i), one, zero) for i in range(2)], axis=1
        )
        result = jnp.dot(jnp.concatenate([times[s, 0], times[s, 1]], axis=0), sel, preferred_element_type=jnp.float32)
        for i in range(2):
            for b in range(2):
                lag[s % 2, m + i, b, 8 : 8 + BLOCK, :] = result[
                    b * BLOCK : (b + 1) * BLOCK, i * LANES : (i + 1) * LANES
                ]

    def fold(s, b):
        sums = {}

        def at(v):
            if not 0 <= v <= BLOCK // 8:
                return blank
            if v not in sums:
                add = lag[s % 2, 0, b, 8 * v : 8 * v + 8, :]
                for m in range(1, 8):
                    add = add + lag[s % 2, m, b, 8 * v + m : 8 * v + m + 8, :]
                sums[v] = add
            return sums[v]

        def line(v):
            if v < -3:
                return blank
            picked = at(v)
            for j in range(1, 4):
                picked = jnp.where(group == j, at(v + j), picked)
            return picked

        for tile in range(3):
            lines = [line(16 * tile - 15 + i) for i in range(16)]
            if tile == 0 and s % 2 == 0:
                lines = lines[4:] + [blank] * 4
            turned = jnp.concatenate(lines, axis=0).T
            folded = (turned[0:32] + turned[32:64]) + (turned[64:96] + turned[96:128])
            part[(tile + 2) % 3, pl.ds(s * 64 + b, 32, stride=2), :] = folded

    def arrive(s):
        load(s).wait()

    arrive(0)
    delay_copy.wait()
    turn_data(0, 0)
    turn_data(0, 1)
    turn_delays(0)
    for s in range(SUBS):
        product(s, 0)
        if s in (1, 3):
            fold(s - 1, 0)
        if s == 2:
            fold(1, 0)
            fold(1, 1)
        product(s, 2)
        if s == 2:
            for copy in small:
                copy.wait()
            pl.semaphore_wait(barrier, NT + 2)
            send_pair(0)
        if s + 1 < SUBS:
            arrive(s + 1)
            turn_data(s + 1, 0)
        product(s, 4)
        if s in (1, 3):
            fold(s - 1, 1)
        product(s, 6)
        if s + 1 < SUBS:
            turn_data(s + 1, 1)
            turn_delays(s + 1)
    fold(SUBS - 1, 0)
    fold(SUBS - 1, 1)
    send_pair(1)

    def forward(pair):
        cut = (core, pl.ds(0, NT), pl.ds(pair * 40, 40))
        return pltpu.make_async_remote_copy(
            src_ref=recv.at[cut], dst_ref=recv.at[cut],
            send_sem=fsend_sem.at[pair], recv_sem=frecv_sem.at[pair],
            device_id={"band": sibling}, device_id_type=MESH,
        )

    def collect(pair):
        all_of(pair).wait_recv()
        forward(pair).start()

    def spread(c, pair):
        def one_block(block, carry):
            early = recv[c, block + 1, pair * 40 + 32 : pair * 40 + 40, :].astype(jnp.float32)
            for h in range(2):
                both = recv[c, block, pair * 40 + h * 16 : pair * 40 + h * 16 + 16, :].astype(jnp.float32)
                for i in range(2):
                    value = both[i * 8 : (i + 1) * 8]
                    if h == 1:
                        moved = pltpu.roll(early, 32, 1) if i == 0 else early
                        value = value + jnp.where(lane >= 96, moved, 0.0)
                    rows[pl.ds((c * SUBS + 2 * pair + i) * 8 * PITCH + 2 * block + h, 8, stride=PITCH), :] = value
            return carry

        lax.fori_loop(0, NT, one_block, 0, unroll=4)

    ahead = lax.broadcasted_iota(jnp.int32, (2 * LANES, LANES), 0) - lax.broadcasted_iota(
        jnp.int32, (2 * LANES, LANES), 1
    )
    for w in range(4):
        inside = (ahead >= 0) & (ahead < width_ref[w])
        window[:, w * LANES : (w + 1) * LANES] = jnp.where(inside, 1.0, 0.0).astype(jnp.bfloat16)
        root = jnp.sqrt(jnp.full((8, LANES), width_ref[w], jnp.int32).astype(jnp.float32))
        roots[:, w * LANES : (w + 1) * LANES] = root

    lane8 = lax.broadcasted_iota(jnp.int32, (2 * ROWS, LANES), 1)

    def trial_sums(owner, g, subs):
        at = owner * 16 + core * 8 + g
        sums = None
        for e in subs:
            shift = off_ref[e, at]
            fine = jnp.bitwise_and(shift, LANES - 1)
            base = (e * 8 + 2 * rel_ref[e, at]) * PITCH + lax.shift_right_logical(shift, 7)
            turn = jnp.bitwise_and(LANES - fine, LANES - 1)
            here, after = [
                jnp.concatenate([rows[pl.ds(base + b * PITCH + next_row, ROWS), :] for b in range(2)], axis=0)
                for next_row in range(2)
            ]
            joined = jnp.where(lane8 >= fine, here, after).astype(jnp.bfloat16)
            moved = pltpu.roll(joined, turn, 1).astype(jnp.float32)
            sums = moved if sums is None else sums + moved
        return sums

    def piece(b, p):
        return {"band": up if b == 0 else down}, pl.ds(p * 4 * ROWS, 4 * ROWS)

    def far(b, p):
        where, cut = piece(b, p)
        return pltpu.make_async_remote_copy(
            src_ref=chunk.at[0, b, cut, :], dst_ref=relay.at[b, cut, :],
            send_sem=zsend_sem.at[0], recv_sem=zrecv_sem.at[2 * b + p],
            device_id=where, device_id_type=MESH,
        )

    def close(side, p):
        where, cut = piece(side, p)
        return pltpu.make_async_remote_copy(
            src_ref=chunk.at[1 + side, side, cut, :], dst_ref=near.at[side, side, cut, :],
            send_sem=zsend_sem.at[0], recv_sem=zrecv_sem.at[4 + 2 * side + p],
            device_id=where, device_id_type=MESH,
        )

    def direct(side):
        return pltpu.make_async_remote_copy(
            src_ref=chunk.at[1 + side, 1 - side], dst_ref=near.at[side, 1 - side],
            send_sem=zsend_sem.at[0], recv_sem=zrecv_sem.at[8 + side],
            device_id={"band": up if side == 0 else down}, device_id_type=MESH,
        )

    def each(g):
        return slice(g * 2 * ROWS, (g + 1) * 2 * ROWS)

    def of(c, pair):
        return (c * SUBS + 2 * pair, c * SUBS + 2 * pair + 1)

    sib = 1 - core

    def first_part(ahead, carry):
        for g in range(8):
            acc[ahead, each(g), :] = trial_sums(lax.rem(z + ahead, 4), g, of(core, 0))
        return carry

    def more_of(ahead, subs):
        for g in range(8):
            acc[ahead, each(g), :] += trial_sums(lax.rem(z + ahead, 4), g, subs)

    rest = {
        2: of(sib, 1),
        1: (2, 3, 6, 7),
        3: of(sib, 0) + (2, 3, 6, 7),
        0: of(sib, 0) + (2, 3, 6, 7),
    }

    def last(ahead, g):
        sums = acc[ahead, each(g), :] + trial_sums(lax.rem(z + ahead, 4), g, rest[ahead])
        return sums[:ROWS], sums[ROWS:]

    def line_of(g):
        return slice(g * ROWS, (g + 1) * ROWS)

    collect(0)
    spread(core, 0)
    lax.fori_loop(0, 4, first_part, 0)
    forward(0).wait()
    spread(sib, 0)
    more_of(2, of(sib, 0))
    collect(1)
    spread(core, 1)
    more_of(2, of(core, 1))
    more_of(1, of(sib, 0))
    forward(1).wait()
    spread(sib, 1)

    for p in range(2):
        for g in range(4 * p, 4 * p + 4):
            sums = last(2, g)
            for b in range(2):
                chunk[0, b, line_of(g), :] = sums[b].astype(jnp.bfloat16)
        for b in range(2):
            far(b, p).start()

    for side in range(2):
        for g in range(8):
            sums = last(1 + 2 * side, g)
            half[side, line_of(g), :] = sums[side]
            chunk[1 + side, 1 - side, line_of(g), :] = sums[1 - side].astype(jnp.bfloat16)
        direct(side).start()

    for g in range(8):
        sums = last(0, g)
        for b in range(2):
            total[b, line_of(g), :] = sums[b]

    for p in range(2):
        cut = slice(p * 4 * ROWS, (p + 1) * 4 * ROWS)
        for side in range(2):
            far(side, p).wait_recv()
            joined = half[side, cut, :] + relay[side, cut, :].astype(jnp.float32)
            chunk[1 + side, side, cut, :] = joined.astype(jnp.bfloat16)
            close(side, p).start()

    for pair in range(2):
        all_of(pair).wait_send()
    for side in range(2):
        direct(side).wait_recv()
        for p in range(2):
            close(side, p).wait_recv()
    pltpu.make_async_remote_copy(
        src_ref=chunk, dst_ref=chunk, send_sem=zsend_sem.at[0], recv_sem=zrecv_sem.at[0],
        device_id={"band": up}, device_id_type=MESH,
    ).wait_send()


def finish(total, near, window, roots, series_ref, peaks_ref, summed):
    for b in range(2):
        summed[b] = (
            total[b] + (near[0, b].astype(jnp.float32) + near[1, b].astype(jnp.float32))
        ) * (1.0 / math.sqrt(CH))

    flat = []
    for row in range(ROWS):
        pieces = [summed[b, pl.ds(row, 8, stride=ROWS), :] for b in range(2)]
        flat.append(jnp.concatenate(pieces, axis=0).astype(jnp.bfloat16))
        for b in range(2):
            series_ref[b, :, row * LANES : (row + 1) * LANES] = pieces[b].astype(jnp.bfloat16)
    flat.append(jnp.zeros((16, LANES), jnp.bfloat16))

    halves = [jnp.concatenate(flat[i : i + ROWS], axis=0) for i in range(2)]
    sums = jnp.dot(jnp.concatenate(halves, axis=1), window[...], preferred_element_type=jnp.float32)
    best = sums[0:16]
    for row in range(1, ROWS):
        best = jnp.maximum(best, sums[row * 16 : (row + 1) * 16])
    for w in range(4):
        cut = slice(w * LANES, (w + 1) * LANES)
        top = jnp.max(best[:, cut].T, axis=0, keepdims=True) / roots[0:1, w * LANES : w * LANES + 16]
        for b in range(2):
            peaks_ref[b, w : w + 1, :] = top[:, b * 8 : (b + 1) * 8]


def local(intensity, fine_delay, span_start, sub_rel, offset, widths):
    vmem = pl.BlockSpec(memory_space=pltpu.VMEM)
    hbm = pl.BlockSpec(memory_space=pltpu.HBM)
    pieces = pl.pallas_call(
        kernel,
        out_shape=(
            jax.ShapeDtypeStruct((2, 8 * ROWS, LANES), jnp.float32),
            jax.ShapeDtypeStruct((2, 2, 8 * ROWS, LANES), jnp.bfloat16),
            jax.ShapeDtypeStruct((2 * LANES, 4 * LANES), jnp.bfloat16),
            jax.ShapeDtypeStruct((8, 4 * LANES), jnp.float32),
        ),
        in_specs=[hbm] * 6,
        out_specs=(vmem,) * 4,
        scratch_shapes=[
            pltpu.VMEM((2, SUBS * CSUB, BLOCK), jnp.bfloat16),
            pltpu.VMEM((SUBS, Q, CSUB), jnp.int32),
            pltpu.SMEM((NT, 32), jnp.int32),
            pltpu.SMEM((8, 64), jnp.int32),
            pltpu.SMEM((8, 64), jnp.int32),
            pltpu.SMEM((4,), jnp.int32),
            pltpu.VMEM((2, 8, 2, BLOCK + 16, LANES), jnp.float32),
            pltpu.VMEM((3, SUBS * Q * 2, LANES), jnp.float32),
            pltpu.VMEM((NT, MSG, LANES), jnp.bfloat16),
            pltpu.VMEM((2, NT + 1, MSG, LANES), jnp.bfloat16),
            pltpu.VMEM((64 * PITCH, LANES), jnp.float32),
            pltpu.VMEM((2, 8 * ROWS, LANES), jnp.bfloat16),
            pltpu.VMEM((3, 2, 8 * ROWS, LANES), jnp.bfloat16),
            pltpu.VMEM((2, 8 * ROWS, LANES), jnp.float32),
            pltpu.VMEM((4, 16 * ROWS, LANES), jnp.float32),
            pltpu.SemaphoreType.DMA((SUBS + 1,)),
            pltpu.SemaphoreType.DMA((4,)),
            pltpu.SemaphoreType.DMA((2,)),
            pltpu.SemaphoreType.DMA((2,)),
            pltpu.SemaphoreType.DMA((2,)),
            pltpu.SemaphoreType.DMA((2,)),
            pltpu.SemaphoreType.DMA((1,)),
            pltpu.SemaphoreType.DMA((10,)),
        ],
        compiler_params=pltpu.CompilerParams(
            collective_id=0, has_side_effects=True, vmem_limit_bytes=VMEM_MIB * 1024 * 1024
        ),
        name="dedisperse",
    )(*[
        pltpu.with_memory_space_constraint(a, pltpu.HBM)
        for a in (intensity, fine_delay, span_start, sub_rel.T, offset.T, widths)
    ])
    series, peaks = pl.pallas_call(
        finish,
        out_shape=(
            jax.ShapeDtypeStruct((2, 8, ROWS * LANES), jnp.bfloat16),
            jax.ShapeDtypeStruct((2, 4, 8), jnp.float32),
        ),
        in_specs=[vmem] * 4,
        out_specs=(vmem, vmem),
        scratch_shapes=[
            pltpu.VMEM((2, 8 * ROWS, LANES), jnp.float32),
        ],
        compiler_params=pltpu.CompilerParams(vmem_limit_bytes=VMEM_MIB * 1024 * 1024),
        name="finish",
    )(*pieces)
    return series, peaks.transpose(0, 2, 1)


def solution(mesh):
    return jax.shard_map(
        local,
        mesh=mesh,
        in_specs=(
            P(None, "band", "trial"),
            P("band", None, None),
            P(),
            P("trial", None),
            P("trial", None),
            P(),
        ),
        out_specs=(P(None, ("trial", "band"), None), P(None, ("trial", "band"), None)),
        check_vma=False,
    )
```
